512 devices in a mesh: facet: 16 (over z, core), sub: 8 (over y), wa: 4 (over x).
Axes of the slice: x: 4, y: 8, z: 8, core: 2. Of those that a mesh axis runs over, the one named last changes fastest.
Arguments:
- facet_data: bfloat16 [16, 512, 2, 8192], P('facet', ('sub', 'wa')), may hold values from -6 to 6
- window: float32 [8192], replicated, may hold values from 0.1 to 1
- screen_phase: float32 [1024, 1024], P('facet'), may hold values from -0.5 to 0.5
- facet_shift: int32 [16], replicated, may hold values from 0 to 1023
- sub_offset: int32 [32], replicated, may hold values from 0 to 8191
- win_start: int32 [16, 32], replicated, may hold values from 0 to 512
- win_extent: int32 [16, 32], replicated, may hold values from 256 to 512, as said below
- owner_slot: int32 [32], replicated, may hold values from 0 to 31, each once
- layer_w: int32 [8], replicated, may hold values from -12 to 12
Outputs:
- layers: bfloat16 [32, 8, 1024, 2, 1024], P('sub', 'wa', 'facet')
The draws below stay inside these ranges and needn't reach their ends.
Inputs may be any that keep to these rules, and one draw needn't show every extreme that they name: win_start[f, j] + win_extent[f, j] <= 1024 for every facet f and subgrid j. A permutation of the subgrids; the subgrid with owner_slot = p belongs to sub index p // 4.
All inputs are finite; a program needn't handle non-finite values.
Results may differ from the reference program's by a relative error of at most 0.008.
Values may be sent and summed in bfloat16 or wider, within the bound.
No kernel may reach another device: no remote copies, remote signals or barrier semaphores. Data moves between devices by JAX's collectives and lax.ppermute only.
A program may use at most 128 MiB of HBM per device.

```python
import math
import jax
import jax.numpy as jnp
from jax import lax

FN = 8192
SG = 1024
NFAC = 16
SUBS = 32
LAYERS = 8
STRIP = 512
EMAX = 512
EMIN = 256


def draw_win_extent(key, part):
    base_key = jax.random.fold_in(key, 11)
    first_key, second_key, third_key = jax.random.split(base_key, 3)
    values = jax.random.randint(first_key, (NFAC, SUBS), EMIN, EMAX + 1)
    chosen = jax.random.randint(second_key, (NFAC,), 0, SUBS)
    column = jax.random.randint(third_key, (), 0, SUBS)
    indices = jnp.arange(SUBS)
    widest = (indices[None, :] == chosen[:, None]) | (indices[None, :] == column)
    return jnp.where(widest, EMAX, values).astype(jnp.int32)


def place_ends(result, key, smallest, largest):
    dims = result.shape
    place = [jax.random.randint(jax.random.fold_in(key, axis), (), 0, dims[axis]) for axis in range(len(dims))]
    result = result.at[tuple(place)].set(smallest)
    longest = dims.index(max(dims))
    place[longest] = (place[longest] + 1) % dims[longest]
    return result.at[tuple(place)].set(largest)


def levels(rng, extent, cuts, low, high):
    def one(dim, parts):
        steps = jax.random.uniform(jax.random.fold_in(jax.random.fold_in(rng, 6), dim), (parts,), jnp.float32, low / len(cuts), high / len(cuts))
        return jnp.repeat(jnp.exp(steps), extent[dim] // parts).reshape((-1,) + (1,) * (len(extent) - dim - 1))

    gain = one(*cuts[0])
    for cut in cuts[1:]:
        gain = gain * one(*cut)
    return gain


def noise(stream_key, extent, scale, most, shards=(), kind=jnp.bfloat16):
    values = scale * jax.random.normal(stream_key, extent, jnp.float32)
    if shards:
        values = values * levels(stream_key, extent, shards, -0.22, 0.18)
    return jnp.clip(values, -most, most).astype(kind)


def setup_inputs(seed: int = 0) -> dict:
    key_list = jax.random.split(jax.random.key(seed), 10)
    return {
        "facet_data": noise(key_list[0], (NFAC, STRIP, 2, FN), 1.0, 6.0, ((0, 16), (1, 32))),
        "window": jnp.clip(jnp.exp(jax.random.uniform(key_list[1], (FN,), jnp.float32, math.log(0.1), math.log(1.0))), 0.1, 1.0),
        "screen_phase": jnp.clip(jax.random.uniform(key_list[2], (SG, SG), jnp.float32, -0.5, 0.5) * levels(key_list[2], (SG, SG), ((0, 16),), -0.4, 0.0), -0.5, 0.5),
        "facet_shift": place_ends(jax.random.randint(key_list[3], (NFAC,), 0, SG), jax.random.fold_in(key_list[3], 1), 0, SG - 1).astype(jnp.int32),
        "sub_offset": place_ends(jax.random.randint(key_list[4], (SUBS,), 0, FN), jax.random.fold_in(key_list[4], 1), 0, FN - 1).astype(jnp.int32),
        "win_start": place_ends(jax.random.randint(key_list[5], (NFAC, SUBS), 0, SG - EMAX + 1), jax.random.fold_in(key_list[5], 1), 0, SG - EMAX).astype(jnp.int32),
        "win_extent": draw_win_extent(jax.random.fold_in(key_list[9], 71), 0),
        "owner_slot": jax.random.permutation(key_list[7], SUBS).astype(jnp.int32),
        "layer_w": place_ends(jax.random.randint(key_list[8], (LAYERS,), -12, 13), jax.random.fold_in(key_list[8], 1), -12, 12).astype(jnp.int32),
    }


def phase_of(products, modulus, sign_value):
    angles = sign_value * 2.0 * math.pi / modulus * (products % modulus).astype(jnp.float32)
    return (jnp.cos(angles), jnp.sin(angles))

def phase_pair(row_ids, col_ids, modulus, sign_value):
    return phase_of(row_ids[:, None] * col_ids[None, :], modulus, sign_value)

def held_bf16(values):
    return lax.optimization_barrier(values.astype(jnp.bfloat16)).astype(jnp.float32)

def precise_dot(left, right):
    return jnp.dot(left, right, precision=lax.Precision.HIGHEST)

def reference(facet_data, window, screen_phase, facet_shift, sub_offset, win_start, win_extent, owner_slot, layer_w):
    signal = facet_data.astype(jnp.float32) * window
    spectrum = jnp.fft.fft(signal[:, :, 0] + 1j * signal[:, :, 1], axis=-1) / math.sqrt(FN)
    columns = jnp.arange(SG, dtype=jnp.int32)
    shift_cos, shift_sin = phase_pair(facet_shift, columns, SG, 1.0)
    strip_ids = jnp.arange(STRIP, dtype=jnp.int32)
    row_cos, row_sin = phase_pair(columns, strip_ids, SG, -1.0)
    row_cos = held_bf16(row_cos)
    row_sin = held_bf16(row_sin)
    fwd_cos, fwd_sin = phase_pair(columns, columns, SG, -1.0)
    fwd_cos = held_bf16(fwd_cos)
    fwd_sin = held_bf16(fwd_sin)

    def one_subgrid(sub_index):
        picked = jnp.take(spectrum, (sub_offset[sub_index] + columns) % FN, axis=2)
        begin_col = win_start[:, sub_index][:, None]
        end_col = begin_col + win_extent[:, sub_index][:, None]
        inside = (columns[None, :] >= begin_col) & (columns[None, :] < end_col)
        part_real = picked.real * shift_cos[:, None, :] - picked.imag * shift_sin[:, None, :]
        part_imag = picked.real * shift_sin[:, None, :] + picked.imag * shift_cos[:, None, :]
        part_real = held_bf16(jnp.where(inside[:, None, :], part_real, 0.0))
        part_imag = held_bf16(jnp.where(inside[:, None, :], part_imag, 0.0))
        summed = (lax.optimization_barrier(jnp.sum(part_real, 0)) + 1j * lax.optimization_barrier(jnp.sum(part_imag, 0))) / math.sqrt(NFAC)
        col_image = jnp.fft.ifft(summed, axis=-1) * math.sqrt(SG)
        q_real = held_bf16(col_image.real)
        q_imag = held_bf16(col_image.imag)
        p_real = (precise_dot(row_cos, q_real) - precise_dot(row_sin, q_imag)) / math.sqrt(STRIP)
        p_imag = (precise_dot(row_sin, q_real) + precise_dot(row_cos, q_imag)) / math.sqrt(STRIP)
        p_real = held_bf16(p_real)
        p_imag = held_bf16(p_imag)

        def one_layer(layer_value):
            turn_angles = layer_value.astype(jnp.float32) * screen_phase
            turn_cos = jnp.cos(turn_angles)
            turn_sin = jnp.sin(turn_angles)
            s_real = held_bf16(p_real * turn_cos - p_imag * turn_sin)
            s_imag = held_bf16(p_real * turn_sin + p_imag * turn_cos)
            o_real = precise_dot(s_real, fwd_cos) - precise_dot(s_imag, fwd_sin)
            o_imag = precise_dot(s_real, fwd_sin) + precise_dot(s_imag, fwd_cos)
            return (jnp.stack([o_real, o_imag], 1) / math.sqrt(SG)).astype(jnp.bfloat16)
        return lax.map(one_layer, layer_w)
    per_subgrid = lax.map(one_subgrid, jnp.arange(SUBS, dtype=jnp.int32))
    return jnp.zeros_like(per_subgrid).at[owner_slot].set(per_subgrid)
```

```python
import functools
import math

import jax
import jax.numpy as jnp
import numpy as np
from jax import lax
from jax.experimental import pallas as pl
from jax.experimental.pallas import tpu as pltpu
from jax.sharding import PartitionSpec as P


def turn(products, modulus):
    return (2.0 * math.pi / modulus) * (products % modulus).astype(jnp.float32)


def iota(shape, dim):
    return lax.broadcasted_iota(jnp.int32, shape, dim)


def times_root(value, power, modulus):
    power %= modulus
    re, im = value
    if power == 0:
        return value
    if 4 * power == modulus:
        return (im, -re)
    if 2 * power == modulus:
        return (-re, -im)
    if 4 * power == 3 * modulus:
        return (-im, re)
    co = math.cos(2.0 * math.pi * power / modulus)
    si = math.sin(2.0 * math.pi * power / modulus)
    return (re * co + im * si, im * co - re * si)


def add(left, right):
    return (left[0] + right[0], left[1] + right[1])


def sub(left, right):
    return (left[0] - right[0], left[1] - right[1])


def small_dft(values):
    count = len(values)
    if count == 1:
        return values
    even = small_dft(values[0::2])
    odd = small_dft(values[1::2])
    odd = [times_root(odd[i], i, count) for i in range(count // 2)]
    return [add(e, o) for e, o in zip(even, odd)] + [sub(e, o) for e, o in zip(even, odd)]


def split_kernel(data_ref, window_ref, twist_ref, out_ref, *, count, inner, lanes):
    for first in range(0, inner, lanes):
        values = []
        for step in range(count):
            cols = slice(step * inner + first, step * inner + first + lanes)
            gain = window_ref[:, cols]
            values.append(
                (
                    data_ref[0, :, cols].astype(jnp.float32) * gain,
                    data_ref[1, :, cols].astype(jnp.float32) * gain,
                )
            )
        result = small_dft(values)
        for part in range(count):
            re, im = result[part]
            co = twist_ref[0, part : part + 1, first : first + lanes]
            si = twist_ref[1, part : part + 1, first : first + lanes]
            out_ref[part, :, first : first + lanes] = (re * co + im * si).astype(jnp.bfloat16)
            out_ref[part, :, inner + first : inner + first + lanes] = (im * co - re * si).astype(
                jnp.bfloat16
            )


def split_rows(data, window, count):
    rows, full = data.shape[1:]
    inner = full // count
    angles = 2.0 * np.pi / full * np.outer(np.arange(count), np.arange(inner))
    twist = jnp.asarray(np.stack([np.cos(angles), np.sin(angles)]).astype(np.float32))
    return pl.pallas_call(
        functools.partial(split_kernel, count=count, inner=inner, lanes=128),
        out_shape=jax.ShapeDtypeStruct((count, rows, 2 * inner), jnp.bfloat16),
    )(data, window[None], twist)


def window_kernel(
    block_ref, alpha_ref, part_ref, table_ref, cos_ref, sin_ref, out_ref, spec_ref, *, rows
):
    facets = part_ref.shape[0] // rows
    blocks = spec_ref.shape[0]
    lanes = spec_ref.shape[2]
    part = part_ref[...]
    for block in range(blocks):
        spec_ref[block] = jnp.dot(
            part,
            table_ref[:, block * lanes : (block + 1) * lanes],
            preferred_element_type=jnp.float32,
        )
    column = (iota((rows, lanes), 1) % (lanes // 2)) * facets + alpha_ref[out_ref.shape[0]]

    def one_slot(slot, carry):
        low = block_ref[slot]
        high = (low + 1) % blocks
        upper = column >= alpha_ref[slot]
        straight = jnp.zeros((rows, lanes), jnp.float32)
        crossed = jnp.zeros((rows, lanes), jnp.float32)
        for facet in range(facets):
            band = slice(facet * rows, (facet + 1) * rows)
            value = jnp.where(upper, spec_ref[low, band], spec_ref[high, band])
            straight += value * cos_ref[slot, facet : facet + 1]
            crossed += value * sin_ref[slot, facet : facet + 1]
        total = straight + pltpu.roll(crossed, lanes // 2, 1)
        out_ref[slot] = total.astype(jnp.bfloat16)
        return carry

    lax.fori_loop(0, out_ref.shape[0], one_slot, 0)


def windowed_sum(parts, table, block, alpha, cos_all, sin_all, rows):
    slots = block.shape[0]
    lanes = cos_all.shape[2]
    smem = pl.BlockSpec(memory_space=pltpu.SMEM)
    vmem = pl.BlockSpec(memory_space=pltpu.VMEM)
    return pl.pallas_call(
        functools.partial(window_kernel, rows=rows),
        out_shape=jax.ShapeDtypeStruct((slots, rows, lanes), jnp.bfloat16),
        in_specs=[smem, smem, vmem, vmem, vmem, vmem],
        out_specs=vmem,
        scratch_shapes=[
            pltpu.VMEM((table.shape[1] // lanes, parts.shape[0], lanes), jnp.float32)
        ],
    )(block, alpha, parts, table, cos_all, sin_all)


def crossed_lanes(value):
    half = value.shape[-1] // 2
    return jnp.concatenate([value[..., half:], -value[..., :half]], -1)


def local(
    facet_data,
    window,
    screen_phase,
    facet_shift,
    sub_offset,
    win_start,
    win_extent,
    owner_slot,
    layer_w,
):
    facets = lax.axis_size("facet")
    teams = lax.axis_size("wa")
    facet_id = lax.axis_index("facet")
    sub_id = lax.axis_index("sub")
    team_id = lax.axis_index("wa")
    rows, full = facet_data.shape[1], facet_data.shape[3]
    band_rows, grid = screen_phase.shape
    total_subs = owner_slot.shape[0]
    strip = rows * lax.axis_size("sub") * teams
    inner = full // facets
    fine = grid // facets
    blocks = full // grid

    parts = split_rows(jnp.transpose(facet_data[0], (1, 0, 2)), window, facets)
    parts = lax.all_to_all(parts, "facet", 0, 0, tiled=True)

    shape = (2 * inner, 2 * inner)
    row_id, col_id = iota(shape, 0), iota(shape, 1)
    freq = (col_id // (2 * fine)) * fine + col_id % fine
    quarter = (inner // 4) * ((col_id // fine) % 2 - row_id // inner)
    spec_table = jnp.cos(turn((row_id % inner) * freq + quarter + inner, inner)).astype(
        jnp.bfloat16
    )

    slot_ids = jnp.arange(total_subs, dtype=jnp.int32)
    chooser = (owner_slot[None, :] == slot_ids[:, None]).astype(jnp.int32)
    offset_slot = jnp.sum(chooser * sub_offset[None, :], axis=1) % full
    start_slot = jnp.sum(win_start[None] * chooser[:, None, :], axis=2)
    extent_slot = jnp.sum(win_extent[None] * chooser[:, None, :], axis=2)
    alpha = offset_slot % grid
    lane = jnp.arange(2 * fine, dtype=jnp.int32)
    column = (lane % fine) * facets + facet_id
    k_id = (column[None, :] - alpha[:, None]) % grid
    k_id = k_id[:, None, :]
    inside = (k_id >= start_slot[:, :, None]) & (k_id < (start_slot + extent_slot)[:, :, None])
    angles = turn(facet_shift[None, :, None] * k_id, grid)
    scale = 1.0 / math.sqrt(full * facets)
    cos_all = jnp.where(inside, jnp.cos(angles) * scale, 0.0)
    sin_all = jnp.where(inside, jnp.sin(angles) * scale, 0.0)
    sin_all = jnp.where(lane[None, None, :] < fine, sin_all, -sin_all)
    summed = windowed_sum(
        parts.reshape(facets * rows, 2 * inner),
        spec_table,
        offset_slot // grid,
        jnp.concatenate([alpha, facet_id[None]]),
        cos_all,
        sin_all,
        rows,
    )
    summed = lax.all_to_all(summed, ("sub", "wa"), 0, 0, tiled=True)

    shape = (grid, 2 * strip)
    row_id, col_id = iota(shape, 0), iota(shape, 1)
    row_table = jnp.cos(
        turn(row_id * (col_id % strip) - (grid // 4) * (col_id // strip) + grid, grid)
    ).astype(jnp.bfloat16)
    mine = summed.reshape(strip, 2 * fine)
    mine = jnp.concatenate([mine, crossed_lanes(mine)], 0)
    turned = jnp.dot(row_table, mine, preferred_element_type=jnp.float32)
    turned = (turned * (1.0 / math.sqrt(strip))).astype(jnp.bfloat16)
    turned = lax.all_to_all(
        turned.reshape(facets, band_rows, 2 * fine), "facet", 0, 0, tiled=True
    )

    shape = (2 * grid, grid)
    row_id, col_id = iota(shape, 0), iota(shape, 1)
    freq = (row_id % fine) * facets + row_id // (2 * fine)
    back_table = jnp.cos(
        turn(freq * col_id + (grid // 4) * ((row_id // fine) % 2), grid)
    ).astype(jnp.bfloat16)
    both = jnp.stack([turned, crossed_lanes(turned)])
    both = jnp.transpose(both, (0, 2, 1, 3)).reshape(2 * band_rows, 2 * grid)
    image = jnp.dot(both, back_table, preferred_element_type=jnp.float32)
    my_alpha = lax.dynamic_index_in_dim(alpha, sub_id * teams + team_id, 0, keepdims=False)
    grid_ids = jnp.arange(grid, dtype=jnp.int32)
    angles = turn(my_alpha * grid_ids, grid)
    cos_row = jnp.cos(angles) * (1.0 / math.sqrt(grid))
    sin_row = jnp.sin(angles) * (1.0 / math.sqrt(grid))
    image_re, image_im = image[:band_rows], image[band_rows:]
    finished = jnp.stack(
        [image_re * cos_row + image_im * sin_row, image_im * cos_row - image_re * sin_row]
    ).astype(jnp.bfloat16)
    finished = lax.all_to_all(
        jnp.broadcast_to(finished[None], (teams, *finished.shape)), "wa", 0, 0, tiled=True
    )

    layer_dev = layer_w.shape[0] // teams
    own_layers = lax.dynamic_slice_in_dim(layer_w, team_id * layer_dev, layer_dev, 0)
    screen = own_layers.astype(jnp.float32)[:, None, None] * screen_phase[None]
    turn_cos, turn_sin = jnp.cos(screen)[None], jnp.sin(screen)[None]
    shape = (2 * grid, 2 * grid)
    row_id, col_id = iota(shape, 0), iota(shape, 1)
    quarter = (grid // 4) * (col_id // grid - row_id // grid)
    forward = jnp.cos(
        turn((row_id % grid) * (col_id % grid) + quarter + grid, grid)
    ).astype(jnp.bfloat16)
    base_re = finished[:, None, 0].astype(jnp.float32)
    base_im = finished[:, None, 1].astype(jnp.float32)
    screened = jnp.concatenate(
        [base_re * turn_cos - base_im * turn_sin, base_re * turn_sin + base_im * turn_cos], 3
    ).astype(jnp.bfloat16)
    result = jnp.dot(
        screened.reshape(-1, 2 * grid), forward, preferred_element_type=jnp.float32
    )
    result = (result * (1.0 / math.sqrt(grid))).astype(jnp.bfloat16)
    return result.reshape(teams, layer_dev, band_rows, 2, grid)


def solution(mesh):
    in_specs = (
        P("facet", ("sub", "wa"), None, None),
        P(),
        P("facet", None),
        P(),
        P(),
        P(),
        P(),
        P(),
        P(),
    )
    out_specs = P("sub", "wa", "facet", None, None)
    return jax.shard_map(local, mesh=mesh, in_specs=in_specs, out_specs=out_specs, check_vma=False)
```

```python
import functools
import math

import jax
import jax.numpy as jnp
import numpy as np
from jax import lax
from jax.experimental import pallas as pl
from jax.experimental.pallas import tpu as pltpu
from jax.sharding import PartitionSpec as P


def turn(products, modulus):
    return (2.0 * math.pi / modulus) * (products % modulus).astype(jnp.float32)


def iota(shape, dim):
    return lax.broadcasted_iota(jnp.int32, shape, dim)


def small_table(rows, cols, modulus, quarter=None):
    angles = 2.0 * np.pi / modulus * ((rows * cols) % modulus)
    if quarter is not None:
        angles = angles + 0.5 * np.pi * quarter
    return (
        jnp.asarray(np.cos(angles).astype(np.float32)),
        jnp.asarray(np.sin(angles).astype(np.float32)),
    )


def product_real(left, right):
    return (left[0] * right[0] - left[1] * right[1]).astype(jnp.bfloat16)


def times_root(value, power, modulus):
    power %= modulus
    re, im = value
    if power == 0:
        return value
    if 4 * power == modulus:
        return (im, -re)
    if 2 * power == modulus:
        return (-re, -im)
    if 4 * power == 3 * modulus:
        return (-im, re)
    co = math.cos(2.0 * math.pi * power / modulus)
    si = math.sin(2.0 * math.pi * power / modulus)
    return (re * co + im * si, im * co - re * si)


def add(left, right):
    return (left[0] + right[0], left[1] + right[1])


def sub(left, right):
    return (left[0] - right[0], left[1] - right[1])


def small_dft(values):
    count = len(values)
    if count == 1:
        return values
    even = small_dft(values[0::2])
    odd = small_dft(values[1::2])
    odd = [times_root(odd[i], i, count) for i in range(count // 2)]
    return [add(e, o) for e, o in zip(even, odd)] + [sub(e, o) for e, o in zip(even, odd)]


def split_kernel(data_ref, window_ref, twist_ref, out_ref, *, count, inner, lanes):
    for first in range(0, inner, lanes):
        values = []
        for step in range(count):
            cols = slice(step * inner + first, step * inner + first + lanes)
            gain = window_ref[:, cols]
            values.append(
                (
                    data_ref[0, :, cols].astype(jnp.float32) * gain,
                    data_ref[1, :, cols].astype(jnp.float32) * gain,
                )
            )
        result = small_dft(values)
        for part in range(count):
            re, im = result[part]
            co = twist_ref[0, part : part + 1, first : first + lanes]
            si = twist_ref[1, part : part + 1, first : first + lanes]
            out_ref[part, :, first : first + lanes] = (re * co + im * si).astype(jnp.bfloat16)
            out_ref[part, :, inner + first : inner + first + lanes] = (im * co - re * si).astype(
                jnp.bfloat16
            )


def split_rows(data, window, count):
    rows, full = data.shape[1:]
    inner = full // count
    angles = 2.0 * np.pi / full * np.outer(np.arange(count), np.arange(inner))
    twist = jnp.asarray(np.stack([np.cos(angles), np.sin(angles)]).astype(np.float32))
    return pl.pallas_call(
        functools.partial(split_kernel, count=count, inner=inner, lanes=128),
        compiler_params=pltpu.CompilerParams(vmem_limit_bytes=16 * 2**20),
        out_shape=jax.ShapeDtypeStruct((count, rows, 2 * inner), jnp.bfloat16),
    )(data, window[None], twist)


def window_kernel(
    block_ref, alpha_ref, part_ref, table_ref, cos_ref, sin_ref, out_ref, spec_ref, *, rows
):
    facets = part_ref.shape[0] // rows
    blocks = spec_ref.shape[0]
    lanes = spec_ref.shape[2]
    part = part_ref[...]
    for block in range(blocks):
        spec_ref[block] = jnp.dot(
            part,
            table_ref[:, block * lanes : (block + 1) * lanes],
            preferred_element_type=jnp.float32,
        )
    column = (iota((rows, lanes), 1) % (lanes // 2)) * facets + alpha_ref[out_ref.shape[0]]

    def one_slot(slot, carry):
        low = block_ref[slot]
        high = (low + 1) % blocks
        upper = column >= alpha_ref[slot]
        straight = jnp.zeros((rows, lanes), jnp.float32)
        crossed = jnp.zeros((rows, lanes), jnp.float32)
        for facet in range(facets):
            band = slice(facet * rows, (facet + 1) * rows)
            value = jnp.where(upper, spec_ref[low, band], spec_ref[high, band])
            straight += value * cos_ref[slot, facet : facet + 1]
            crossed += value * sin_ref[slot, facet : facet + 1]
        total = straight + pltpu.roll(crossed, lanes // 2, 1)
        out_ref[slot] = total.astype(jnp.bfloat16)
        return carry

    lax.fori_loop(0, out_ref.shape[0], one_slot, 0, unroll=4)


def windowed_sum(parts, table, block, alpha, cos_all, sin_all, rows):
    slots = block.shape[0]
    lanes = cos_all.shape[2]
    smem = pl.BlockSpec(memory_space=pltpu.SMEM)
    vmem = pl.BlockSpec(memory_space=pltpu.VMEM)
    return pl.pallas_call(
        functools.partial(window_kernel, rows=rows),
        compiler_params=pltpu.CompilerParams(vmem_limit_bytes=16 * 2**20),
        out_shape=jax.ShapeDtypeStruct((slots, rows, lanes), jnp.bfloat16),
        in_specs=[smem, smem, vmem, vmem, vmem, vmem],
        out_specs=vmem,
        scratch_shapes=[
            pltpu.VMEM((table.shape[1] // lanes, parts.shape[0], lanes), jnp.float32)
        ],
    )(block, alpha, near(parts), near(table), cos_all, sin_all)


def image_kernel(part_ref, table_ref, phase_ref, out_ref):
    facets, rows, lanes = part_ref.shape
    ways, _, width = table_ref.shape
    sign = jnp.where(iota((rows, lanes), 1) < lanes // 2, 1.0, -1.0)
    outs = []
    for way in range(ways):
        plain, crossed = [], []
        for facet in range(way, facets, ways):
            piece = part_ref[facet]
            turned = pltpu.roll(piece.astype(jnp.float32), lanes // 2, 1) * sign
            plain.append(piece)
            crossed.append(turned.astype(jnp.bfloat16))
        both = jnp.concatenate(
            [jnp.concatenate(plain, 1), jnp.concatenate(crossed, 1)], 0
        )
        result = jnp.dot(both, table_ref[way], preferred_element_type=jnp.float32)
        outs.append((result[:rows], result[rows:]))
    for half, (re, im) in enumerate([add(*outs), sub(*outs)]):
        co = phase_ref[0, half : half + 1]
        si = phase_ref[1, half : half + 1]
        cols = slice(half * width, (half + 1) * width)
        re, im = (
            (re * co + im * si).astype(jnp.bfloat16),
            (im * co - re * si).astype(jnp.bfloat16),
        )
        out_ref[0, :, cols] = re
        out_ref[1, :, cols] = im


def column_image(parts, table, phase):
    rows = parts.shape[1]
    vmem = pl.BlockSpec(memory_space=pltpu.VMEM)
    return pl.pallas_call(
        image_kernel,
        in_specs=[vmem, vmem, vmem],
        compiler_params=pltpu.CompilerParams(vmem_limit_bytes=16 * 2**20),
        out_shape=jax.ShapeDtypeStruct((2, rows, table.shape[0] * table.shape[2]), jnp.bfloat16),
    )(near(parts), near(table), phase)


def layer_kernel(slot_ref, *refs, count, scale):
    for step in range(count):

        @pl.when(pl.program_id(0) == step)
        def one_slot():
            layer_slot(refs[step], *refs[count : count + 3], refs[-1], scale)


def layer_slot(image_ref, cos_ref, sin_ref, table_ref, out_ref, scale):
    layers, rows, grid = cos_ref.shape
    ways, size, width = table_ref.shape
    half = width // 2
    run = size // 4
    re_all, im_all = [], []
    base_re = image_ref[0].astype(jnp.float32)
    base_im = image_ref[1].astype(jnp.float32)
    for layer in range(layers):
        co, si = cos_ref[layer], sin_ref[layer]
        re_all.append((base_re * co - base_im * si).astype(jnp.bfloat16))
        im_all.append((base_re * si + base_im * co).astype(jnp.bfloat16))
    re_all = jnp.concatenate(re_all, 0)
    im_all = jnp.concatenate(im_all, 0)
    values = []
    for way in range(ways):
        left = []
        for plane in (re_all, im_all):
            for first in range(0, grid, ways * run):
                left.append(plane[:, first + way * run : first + (way + 1) * run])
        result = jnp.dot(
            jnp.concatenate(left, 1), table_ref[way], preferred_element_type=jnp.float32
        )
        values.append((result[:, :half] * scale, result[:, half:] * scale))
    for turn_id, pair in enumerate(small_dft(values)):
        cols = slice(turn_id * half, (turn_id + 1) * half)
        for layer in range(layers):
            band = slice(layer * rows, (layer + 1) * rows)
            for plane in range(2):
                out_ref[0, layer, :, plane, cols] = pair[plane][band].astype(jnp.bfloat16)


def layer_images(slot_ids, images, cos_all, sin_all, table, earlier, slots):
    layers, rows, grid = cos_all.shape
    count = len(images)
    args = [near(value) for value in (*images, cos_all, sin_all, table)]
    in_specs = [pl.BlockSpec(memory_space=pltpu.VMEM)] * len(args)
    aliases = {}
    if earlier is not None:
        in_specs.append(pl.BlockSpec(memory_space=pl.ANY))
        aliases = {len(args) + 1: 0}
        args.append(earlier)
    return pl.pallas_call(
        functools.partial(layer_kernel, count=count, scale=1.0 / math.sqrt(grid)),
        grid_spec=pltpu.PrefetchScalarGridSpec(
            num_scalar_prefetch=1,
            grid=(count,),
            in_specs=in_specs,
            out_specs=pl.BlockSpec(
                (1, layers, rows, 2, grid), lambda step, slot_ref: (slot_ref[step], 0, 0, 0, 0)
            ),
        ),
        compiler_params=pltpu.CompilerParams(vmem_limit_bytes=16 * 2**20),
        out_shape=jax.ShapeDtypeStruct((slots, layers, rows, 2, grid), jnp.bfloat16),
        input_output_aliases=aliases,
    )(slot_ids, *args)


def near(value):
    return pltpu.with_memory_space_constraint(value, pltpu.VMEM)


def crossed_lanes(value):
    half = value.shape[-1] // 2
    return jnp.concatenate([value[..., half:], -value[..., :half]], -1)


def local(
    facet_data,
    window,
    screen_phase,
    facet_shift,
    sub_offset,
    win_start,
    win_extent,
    owner_slot,
    layer_w,
):
    facets = lax.axis_size("facet")
    teams = lax.axis_size("wa")
    facet_id = lax.axis_index("facet")
    sub_id = lax.axis_index("sub")
    team_id = lax.axis_index("wa")
    rows, full = facet_data.shape[1], facet_data.shape[3]
    band_rows, grid = screen_phase.shape
    total_subs = owner_slot.shape[0]
    strip = rows * lax.axis_size("sub") * teams
    inner = full // facets
    fine = grid // facets
    blocks = full // grid

    parts = split_rows(jnp.transpose(facet_data[0], (1, 0, 2)), window, facets)
    parts = lax.all_to_all(parts, "facet", 0, 0, tiled=True)

    low = 32
    cols = np.arange(2 * inner)
    col_part = (cols // fine) % 2
    freq = (cols // (2 * fine)) * fine + cols % fine
    first = small_table(
        np.arange(0, inner, low)[None, :, None, None],
        freq,
        inner,
        col_part - np.arange(2)[:, None, None, None],
    )
    spec_table = product_real(
        first, small_table(np.arange(low)[None, None, :, None], freq, inner)
    ).reshape(2 * inner, 2 * inner)

    slot_ids = jnp.arange(total_subs, dtype=jnp.int32)
    chooser = (owner_slot[None, :] == slot_ids[:, None]).astype(jnp.int32)
    offset_slot = jnp.sum(chooser * sub_offset[None, :], axis=1) % full
    start_slot = jnp.sum(win_start[None] * chooser[:, None, :], axis=2)
    extent_slot = jnp.sum(win_extent[None] * chooser[:, None, :], axis=2)
    alpha = offset_slot % grid
    lane = jnp.arange(2 * fine, dtype=jnp.int32)
    column = (lane % fine) * facets + facet_id
    k_id = (column[None, :] - alpha[:, None]) % grid
    k_id = k_id[:, None, :]
    inside = (k_id >= start_slot[:, :, None]) & (k_id < (start_slot + extent_slot)[:, :, None])
    angles = turn(facet_shift[None, :, None] * k_id, grid)
    scale = 1.0 / math.sqrt(full * facets)
    cos_all = jnp.where(inside, jnp.cos(angles) * scale, 0.0)
    sin_all = jnp.where(inside, jnp.sin(angles) * scale, 0.0)
    sin_all = jnp.where(lane[None, None, :] < fine, sin_all, -sin_all)
    cols = np.arange(2 * strip)
    first = small_table(
        np.arange(0, grid, low)[:, None, None], cols % strip, grid, -(cols // strip)
    )
    row_table = product_real(
        first, small_table(np.arange(low)[None, :, None], cols % strip, grid)
    ).reshape(grid, 2 * strip)
    ways = 4
    run = grid // 2 // ways
    lanes = np.arange(grid // 2)
    cols = ways * (lanes % run) + lanes // run
    first = small_table(
        np.arange(facets).reshape(-1, 2).T[:, :, None, None, None],
        cols,
        grid,
        np.arange(2)[None, None, :, None, None],
    )
    back_table = product_real(
        first, small_table(facets * np.arange(fine)[None, None, None, :, None], cols, grid)
    ).reshape(2, grid, grid // 2)
    my_alpha = lax.dynamic_index_in_dim(alpha, sub_id * teams + team_id, 0, keepdims=False)
    v_ids = jnp.asarray(np.stack([cols, cols + grid // 2]), jnp.int32)
    angles = turn(my_alpha * v_ids, grid)
    phase = jnp.stack([jnp.cos(angles), jnp.sin(angles)]) * (1.0 / math.sqrt(grid))
    layer_dev = layer_w.shape[0] // teams
    own_layers = lax.dynamic_slice_in_dim(layer_w, team_id * layer_dev, layer_dev, 0)
    placed = jnp.transpose(
        screen_phase.reshape(band_rows, 2, run, ways), (0, 1, 3, 2)
    ).reshape(band_rows, grid)
    cols = np.arange(grid // 2)
    col_part = cols // (grid // ways)
    cols = cols % (grid // ways)
    step = 16
    v_high = np.arange(0, grid // 2, ways * step) + np.array([[0], [grid // 2]])
    first = small_table(
        v_high[None, None, :, :, None, None],
        cols,
        grid,
        col_part - np.arange(2)[None, :, None, None, None, None],
    )
    v_low = ways * np.arange(step) + np.arange(ways)[:, None]
    forward = product_real(
        first, small_table(v_low[:, None, None, None, :, None], cols, grid)
    ).reshape(ways, grid // 2, grid // 2)
    parts, row_table, phase = lax.optimization_barrier((parts, row_table, phase))
    summed = windowed_sum(
        parts.reshape(facets * rows, 2 * inner),
        spec_table,
        offset_slot // grid,
        jnp.concatenate([alpha, facet_id[None]]),
        cos_all,
        sin_all,
        rows,
    )
    summed = lax.all_to_all(summed, ("sub", "wa"), 0, 0, tiled=True)

    mine = summed.reshape(strip, 2 * fine)
    mine = jnp.concatenate([mine, crossed_lanes(mine)], 0)
    turned = jnp.dot(row_table, mine, preferred_element_type=jnp.float32)
    turned = (turned * (1.0 / math.sqrt(strip))).astype(jnp.bfloat16)
    turned = lax.all_to_all(
        turned.reshape(facets, band_rows, 2 * fine), "facet", 0, 0, tiled=True
    )
    screen = own_layers.astype(jnp.float32)[:, None, None] * placed[None]
    turn_cos, turn_sin = jnp.cos(screen), jnp.sin(screen)
    turned, back_table, forward, turn_cos, turn_sin = lax.optimization_barrier(
        (turned, back_table, forward, turn_cos, turn_sin)
    )
    image = column_image(turned, back_table, phase)
    images = [image] + [
        lax.ppermute(image, "wa", [(i, (i + hop) % teams) for i in range(teams)])
        for hop in range(1, teams)
    ]
    slot_ids = (team_id - jnp.arange(teams, dtype=jnp.int32)) % teams
    shared = (turn_cos, turn_sin, forward)
    result = layer_images(slot_ids[:1], images[:1], *shared, None, teams)
    return layer_images(slot_ids[1:], images[1:], *shared, result, teams)


def solution(mesh):
    in_specs = (
        P("facet", ("sub", "wa"), None, None),
        P(),
        P("facet", None),
        P(),
        P(),
        P(),
        P(),
        P(),
        P(),
    )
    out_specs = P("sub", "wa", "facet", None, None)
    return jax.shard_map(local, mesh=mesh, in_specs=in_specs, out_specs=out_specs, check_vma=False)
```
